32 devices in a mesh: row: 4 (over y, x), dict: 8 (over z, core).
Axes of the slice: x: 2, y: 2, z: 4, core: 2. Of those that a mesh axis runs over, the one named last changes fastest.
Arguments:
- activations: bfloat16 [4096, 4096], P(('row', 'dict')), may hold values from -6 to 6
- block_ids: int32 [4096, 4], P(('row', 'dict')), may hold values from 0 to 15, all different within a row; in each aligned block of 128 rows (0 to 127, 128 to 255, ...) at most 48 rows name the same one
- enc_weight: bfloat16 [2048, 4096], P('dict'), may hold values from -0.09375 to 0.09375
- enc_bias: float32 [2048], P('dict'), may hold values from -3 to 3
- dec_weight: bfloat16 [2048, 4096], P('dict'), may hold values from -0.25 to 0.25
- dec_bias: float32 [4096], replicated, may hold values from -3 to 3
Outputs:
- rebuilt: bfloat16 [4096, 4096], P(('row', 'dict'))
- enc_grad: bfloat16 [4096, 2048], P('row', 'dict')
- dec_grad: bfloat16 [4096, 2048], P('row', 'dict')
The draws below stay inside these ranges and needn't reach their ends.
Inputs may be any that keep to these rules, and one draw needn't show every extreme that they name: `block_ids`: each row names 4 different blocks. Among the rows of one device no block is named by more than 48 rows, and some block is named by exactly 48.
All inputs are finite; a program needn't handle non-finite values.
Results may differ from the reference program's by a relative error of at most 0.0059.
Values may be sent and summed in bfloat16 or wider, within the bound.
A program may use at most 128 MiB of HBM per device.

```python
import math
import jax
import jax.numpy as jnp
import numpy as np
from jax import lax

D = 4096
BS = 128
K = 4
TOK_DEV = 128
NB = 16
LATENTS = 2048
MOST = 48
ROWS = 4096
N_ROW = 4
N_DICT = 8


def shard_levels(key, dims, cuts, smallest, top_value):
    def one(axis_at, blocks):
        heights = jax.random.uniform(jax.random.fold_in(jax.random.fold_in(key, 6), axis_at), (blocks,), jnp.float32, smallest / len(cuts), top_value / len(cuts))
        return jnp.repeat(jnp.exp(heights), dims[axis_at] // blocks).reshape((-1,) + (1,) * (len(dims) - axis_at - 1))

    factor_of = one(*cuts[0])
    for cut in cuts[1:]:
        factor_of = factor_of * one(*cut)
    return factor_of


def deal_out(own_key, own, number, rows, count, top, most, skew):
    sequence = jax.random.permutation(own_key, count)
    packed, usual = shares(count, rows * top, most, skew, True), shares(count, rows * top, most, skew, False)
    places = jnp.arange(count)

    def named(lengths, turn):
        used = int((lengths > 0).sum())
        fixed = max(1, used // 4)
        passed = fixed + (places - fixed + turn * (used - fixed)) % max(1, count - fixed)
        return jnp.zeros((count,), jnp.int32).at[sequence[jnp.where(places < fixed, places, passed)]].set(jnp.asarray(lengths, jnp.int32))

    lengths = jnp.where(number % 4 == 0, named(packed, number // 4), named(usual, number - number // 4 - 1))
    mixed = jax.random.permutation(jax.random.fold_in(own, 3), count)
    giver, taker = mixed[0:count // 2 * 2:2], mixed[1:count // 2 * 2:2]
    room = jnp.minimum(lengths[giver] - 1, most - lengths[taker]) // 2
    room = jnp.where((giver == sequence[0]) | (taker == sequence[0]) | (lengths[taker] == 0), 0, jnp.maximum(room, 0))
    passed = jax.random.randint(jax.random.fold_in(own, 4), (count // 2,), 0, 1 << 20) % (room + 1)
    lengths = lengths.at[giver].add(-passed).at[taker].add(passed)
    labels = jnp.searchsorted(jnp.cumsum(lengths), jnp.arange(rows * top), side="right").astype(jnp.int32)
    listing = labels.reshape(top, rows).T
    listing = listing[jax.random.permutation(jax.random.fold_in(own, 1), rows)]
    turn = jax.random.randint(jax.random.fold_in(own, 2), (rows, 1), 0, top)
    return jnp.take_along_axis(listing, (jnp.arange(top)[None, :] + turn) % top, axis=1)


def shares(amount, total, bound, slope, full):
    portions = [(1 << 20) // math.isqrt(grade ** slope) + 1 for grade in range(1, amount + 1)]
    largest = bound if full else min(bound, max(-(-total // amount), total * portions[0] // sum(portions)))
    least = 1 if total - largest >= amount - 1 else 0
    given, rest = [largest] + [least] * (amount - 1), total - largest - least * (amount - 1)
    while rest > 0:
        free = [i for i in range(1, amount) if given[i] < largest] or [i for i in range(1, amount) if given[i] < bound]
        pool, budget = sum([portions[i] for i in free]), rest
        for i in free:
            addition = min(bound - given[i], max(1, budget * portions[i] // pool), rest)
            given[i] = given[i] + addition
            rest = rest - addition
    return np.array(given)


def scatter_about(key, extent, spread, bound, cuts=(), kind=jnp.bfloat16):
    array = jax.random.normal(key, extent, jnp.float32) * spread
    if len(cuts) > 0:
        array = shard_levels(key, extent, cuts, -0.22, 0.18) * array
    return jnp.clip(array, min=-bound, max=bound).astype(kind)


def setup_inputs(seed: int = 0) -> dict:
    splits = jax.random.split(jax.random.key(seed), 7)
    activations = scatter_about(splits[0], (ROWS, D), 1.0, 6.0, ((0, 32),))
    block_ids_keys = jax.random.split(jax.random.fold_in(splits[1], 1), ROWS // TOK_DEV)
    block_ids_turns = jax.random.permutation(jax.random.fold_in(splits[1], 3), ROWS // TOK_DEV)
    block_ids = jax.vmap(lambda own, number: deal_out(jax.random.fold_in(splits[1], 2), own, number, TOK_DEV, NB, K, MOST, 2))(block_ids_keys, block_ids_turns).reshape((ROWS, K))
    enc_weight = scatter_about(splits[2], (LATENTS, D), D ** -0.5, 0.09375, ((0, 8),))
    enc_bias = scatter_about(splits[3], (LATENTS,), 0.5, 3.0, ((0, 8),), jnp.float32)
    dec_weight = scatter_about(splits[4], (LATENTS, D), (K * BS) ** -0.5, 0.25, ((0, 8),))
    dec_bias = scatter_about(splits[5], (D,), 0.5, 3.0, (), jnp.float32)
    return dict(activations=activations, block_ids=block_ids, enc_weight=enc_weight, enc_bias=enc_bias, dec_weight=dec_weight, dec_bias=dec_bias)


LOSS_SCALE = 0.03125

def gelu_tanh(values):
    return jax.nn.gelu(values, approximate=True)

def gelu_grad(pre_act, upstream):
    return jax.vjp(gelu_tanh, pre_act)[1](upstream)[0]

def reference(activations, block_ids, enc_weight, enc_bias, dec_weight, dec_bias):
    total_rows, features = activations.shape
    blocks = enc_weight.shape[0] // BS
    capacity = N_ROW * N_DICT * MOST
    shifted = (activations.astype(jnp.float32) - dec_bias[None, :]).astype(jnp.bfloat16)
    padded = jnp.concatenate([shifted, jnp.zeros((1, features), jnp.bfloat16)], axis=0)
    enc_blocks = enc_weight.reshape(blocks, BS, features)
    dec_blocks = dec_weight.reshape(blocks, BS, features)
    bias_blocks = enc_bias.reshape(blocks, BS)

    def encode(block_index):
        chosen_mask = jnp.any(block_ids == block_index, axis=1)
        chosen = jnp.nonzero(chosen_mask, size=capacity, fill_value=total_rows)[0].astype(jnp.int32)
        gathered = padded[chosen]
        pre_act = jnp.dot(gathered, enc_blocks[block_index].T, preferred_element_type=jnp.float32)
        pre_act = pre_act + bias_blocks[block_index][None, :]
        return (chosen, gathered, pre_act)

    def forward(running, block_index):
        chosen, gathered, pre_act = encode(block_index)
        latent = gelu_tanh(pre_act).astype(jnp.bfloat16)
        partial_value = jnp.dot(latent, dec_blocks[block_index], preferred_element_type=jnp.float32).astype(jnp.bfloat16)
        return (running.at[chosen].add(partial_value.astype(jnp.float32), mode='drop'), None)
    initial = jnp.broadcast_to(dec_bias[None, :], (total_rows, features)).astype(jnp.float32)
    recon_full, _ = lax.scan(forward, initial, jnp.arange(blocks, dtype=jnp.int32))
    residual = ((recon_full - activations.astype(jnp.float32)) * LOSS_SCALE).astype(jnp.bfloat16)
    residual_padded = jnp.concatenate([residual, jnp.zeros((1, features), jnp.bfloat16)], axis=0)

    def backward(running, block_index):
        chosen, gathered, pre_act = encode(block_index)
        latent = gelu_tanh(pre_act).astype(jnp.bfloat16)
        residual_rows = residual_padded[chosen]
        upstream = jnp.dot(residual_rows, dec_blocks[block_index].T, preferred_element_type=jnp.float32)
        latent_grad = gelu_grad(pre_act, upstream).astype(jnp.bfloat16)
        dec_part = jnp.dot(latent.T, residual_rows, preferred_element_type=jnp.float32)
        enc_part = jnp.dot(latent_grad.T, gathered, preferred_element_type=jnp.float32)
        return (running, (enc_part.astype(jnp.bfloat16), dec_part.astype(jnp.bfloat16)))
    _, (enc_parts, dec_parts) = lax.scan(backward, jnp.zeros((), jnp.float32), jnp.arange(blocks, dtype=jnp.int32))
    enc_grad = jnp.transpose(enc_parts, (2, 0, 1)).reshape(features, blocks * BS)
    dec_grad = jnp.transpose(dec_parts, (2, 0, 1)).reshape(features, blocks * BS)
    return (recon_full.astype(jnp.bfloat16), enc_grad, dec_grad)
```

```python
import jax
import jax.numpy as jnp
from jax import lax
from jax.sharding import PartitionSpec as P

BS = 128
K = 4


LOSS_SCALE = 0.03125


def gelu_tanh(values):
    return jax.nn.gelu(values, approximate=True)


def gelu_grad(pre_act, upstream):
    return jax.vjp(gelu_tanh, pre_act)[1](upstream)[0]


def slot_plan(block_ids, groups, total_blocks, slot_depth):
    rows_total = block_ids.shape[0]
    picks = block_ids.shape[1]
    per_group = rows_total // groups
    flat_ids = block_ids.reshape(groups, per_group * picks)
    onehot = (
        flat_ids[:, :, None] == jnp.arange(total_blocks, dtype=jnp.int32)[None, None, :]
    ).astype(jnp.int32)
    rank_in_block = jnp.sum((jnp.cumsum(onehot, axis=1) - 1) * onehot, axis=2)
    group_index = jnp.arange(groups, dtype=jnp.int32)[:, None]
    target = ((flat_ids * groups + group_index) * slot_depth + rank_in_block).reshape(-1)
    source_row = jnp.arange(rows_total * picks, dtype=jnp.int32) // picks
    filled = (
        jnp.full((total_blocks * groups * slot_depth,), rows_total, jnp.int32)
        .at[target]
        .set(source_row)
    )
    return (target, filled)


def pack_rows(values, filled, shape):
    padded = jnp.concatenate([values, jnp.zeros((1, values.shape[1]), values.dtype)], axis=0)
    return padded[filled].reshape(shape)


def on_device(activations, block_ids, enc_weight, enc_bias, dec_weight, dec_bias):
    rows_here, features = activations.shape
    dict_size = lax.axis_size("dict")
    row_size = lax.axis_size("row")
    local_latents = enc_weight.shape[0]
    block_count = local_latents // BS
    total_blocks = block_count * dict_size
    slot_depth = max(2, 3 * rows_here * K // (2 * total_blocks))
    enc_blocks = enc_weight.reshape(block_count, BS, features)
    dec_blocks = dec_weight.reshape(block_count, BS, features)
    bias_blocks = enc_bias.reshape(block_count, BS)
    shifted = (activations.astype(jnp.float32) - dec_bias[None, :]).astype(jnp.bfloat16)
    target, filled = slot_plan(block_ids, 1, total_blocks, slot_depth)
    outgoing = pack_rows(shifted, filled, (dict_size, block_count, slot_depth, features))
    encode_received = lax.all_to_all(outgoing, "dict", split_axis=0, concat_axis=0, tiled=True)
    pre_act = jnp.einsum(
        "sbmd,bcd->sbmc", encode_received, enc_blocks, preferred_element_type=jnp.float32
    )
    pre_act = pre_act + bias_blocks[None, :, None, :]
    encode_latent = gelu_tanh(pre_act).astype(jnp.bfloat16)
    partial_value = jnp.einsum(
        "sbmc,bcd->sbmd", encode_latent, dec_blocks, preferred_element_type=jnp.float32
    ).astype(jnp.bfloat16)
    partial_value, pre_act, latent, received = (
        partial_value,
        pre_act,
        encode_latent,
        encode_received,
    )
    returned = lax.all_to_all(partial_value, "dict", split_axis=0, concat_axis=0, tiled=True)
    slot_parts = (
        returned.reshape(-1, features)[target].astype(jnp.float32).reshape(rows_here, K, features)
    )
    recon_full = dec_bias[None, :] + jnp.sum(slot_parts, axis=1)
    rebuilt = recon_full.astype(jnp.bfloat16)
    residual = ((recon_full - activations.astype(jnp.float32)) * LOSS_SCALE).astype(jnp.bfloat16)
    residual_sent = pack_rows(residual, filled, (dict_size, block_count, slot_depth, features))
    residual_held = lax.all_to_all(residual_sent, "dict", split_axis=0, concat_axis=0, tiled=True)
    upstream = jnp.einsum(
        "sbmd,bcd->sbmc", residual_held, dec_blocks, preferred_element_type=jnp.float32
    )
    latent_grad = gelu_grad(pre_act, upstream).astype(jnp.bfloat16)
    product = jnp.einsum(
        "sbmc,sbmd->dbc", latent, residual_held, preferred_element_type=jnp.float32
    )
    dec_grad = lax.psum_scatter(
        product.reshape(features // row_size * lax.axis_size("row"), local_latents),
        "row",
        scatter_dimension=0,
        tiled=True,
    ).astype(jnp.bfloat16)
    product = jnp.einsum(
        "sbmc,sbmd->dbc", latent_grad, received, preferred_element_type=jnp.float32
    )
    enc_grad = lax.psum_scatter(
        product.reshape(features // row_size * lax.axis_size("row"), local_latents),
        "row",
        scatter_dimension=0,
        tiled=True,
    ).astype(jnp.bfloat16)
    return (rebuilt, enc_grad, dec_grad)


def gelu_and_slope(values):
    inner = 0.7978845608 * (values + 0.044715 * values * values * values)
    bend = jnp.tanh(inner)
    half = 0.5 * (1.0 + bend)
    slope = half + 0.5 * values * (1.0 - bend * bend) * 0.7978845608 * (
        1.0 + 3.0 * 0.044715 * values * values
    )
    return values * half, slope


def dense_on_device(activations, block_ids, enc_weight, enc_bias, dec_weight, dec_bias):
    local_latents = enc_weight.shape[0]
    block_count = local_latents // BS
    me = lax.axis_index("dict")
    shifted = (activations.astype(jnp.float32) - dec_bias[None, :]).astype(jnp.bfloat16)
    ids = lax.all_gather(block_ids, "dict", axis=0, tiled=True)
    held = lax.all_gather(shifted, "dict", axis=0, tiled=True)
    mine = me * block_count + jnp.arange(local_latents, dtype=jnp.int32) // BS
    mask = jnp.any(ids[:, :, None] == mine[None, None, :], axis=1)
    pre_act = lax.dot_general(
        held, enc_weight, (((1,), (1,)), ((), ())), preferred_element_type=jnp.float32
    )
    pre_act = pre_act + enc_bias[None, :]
    value, slope = gelu_and_slope(pre_act)
    latent = jnp.where(mask, value, 0.0).astype(jnp.bfloat16)
    slope = jnp.where(mask, slope, 0.0)
    partial_sum = jnp.dot(latent, dec_weight, preferred_element_type=jnp.float32)
    total = lax.psum_scatter(
        partial_sum.astype(jnp.bfloat16), "dict", scatter_dimension=0, tiled=True
    )
    recon_full = dec_bias[None, :] + total.astype(jnp.float32)
    rebuilt = recon_full.astype(jnp.bfloat16)
    residual = ((recon_full - activations.astype(jnp.float32)) * LOSS_SCALE).astype(jnp.bfloat16)
    residual_held = lax.all_gather(residual, "dict", axis=0, tiled=True)
    upstream = lax.dot_general(
        residual_held, dec_weight, (((1,), (1,)), ((), ())), preferred_element_type=jnp.float32
    )
    latent_grad = (slope * upstream).astype(jnp.bfloat16)

    def reduced(rows_by_features, rows_by_latents):
        product = lax.dot_general(
            rows_by_features,
            rows_by_latents,
            (((0,), (0,)), ((), ())),
            preferred_element_type=jnp.float32,
        )
        return lax.psum_scatter(product, "row", scatter_dimension=0, tiled=True).astype(
            jnp.bfloat16
        )

    dec_grad = reduced(residual_held, latent)
    enc_grad = reduced(held, latent_grad)
    return (rebuilt, enc_grad, dec_grad)


def solution(mesh):
    few_blocks = mesh.shape["dict"] <= 8
    return jax.shard_map(
        dense_on_device if few_blocks else on_device,
        mesh=mesh,
        in_specs=(
            P(("row", "dict"), None),
            P(("row", "dict"), None),
            P("dict", None),
            P("dict"),
            P("dict", None),
            P(),
        ),
        out_specs=(P(("row", "dict"), None), P("row", "dict"), P("row", "dict")),
        check_vma=False,
    )
```

```python
import jax
import jax.numpy as jnp
from jax import lax
from jax.experimental import pallas as pl
from jax.experimental.pallas import tpu as pltpu
from jax.sharding import PartitionSpec as P

BS = 128
K = 4


LOSS_SCALE = 0.03125


def gelu_tanh(values):
    return jax.nn.gelu(values, approximate=True)


def gelu_grad(pre_act, upstream):
    return jax.vjp(gelu_tanh, pre_act)[1](upstream)[0]


def slot_plan(block_ids, groups, total_blocks, slot_depth):
    rows_total = block_ids.shape[0]
    picks = block_ids.shape[1]
    per_group = rows_total // groups
    flat_ids = block_ids.reshape(groups, per_group * picks)
    onehot = (
        flat_ids[:, :, None] == jnp.arange(total_blocks, dtype=jnp.int32)[None, None, :]
    ).astype(jnp.int32)
    rank_in_block = jnp.sum((jnp.cumsum(onehot, axis=1) - 1) * onehot, axis=2)
    group_index = jnp.arange(groups, dtype=jnp.int32)[:, None]
    target = ((flat_ids * groups + group_index) * slot_depth + rank_in_block).reshape(-1)
    source_row = jnp.arange(rows_total * picks, dtype=jnp.int32) // picks
    filled = (
        jnp.full((total_blocks * groups * slot_depth,), rows_total, jnp.int32)
        .at[target]
        .set(source_row)
    )
    return (target, filled)


def pack_rows(values, filled, shape):
    padded = jnp.concatenate([values, jnp.zeros((1, values.shape[1]), values.dtype)], axis=0)
    return padded[filled].reshape(shape)


def on_device(activations, block_ids, enc_weight, enc_bias, dec_weight, dec_bias):
    rows_here, features = activations.shape
    dict_size = lax.axis_size("dict")
    row_size = lax.axis_size("row")
    local_latents = enc_weight.shape[0]
    block_count = local_latents // BS
    total_blocks = block_count * dict_size
    slot_depth = max(2, 3 * rows_here * K // (2 * total_blocks))
    enc_blocks = enc_weight.reshape(block_count, BS, features)
    dec_blocks = dec_weight.reshape(block_count, BS, features)
    bias_blocks = enc_bias.reshape(block_count, BS)
    shifted = (activations.astype(jnp.float32) - dec_bias[None, :]).astype(jnp.bfloat16)
    target, filled = slot_plan(block_ids, 1, total_blocks, slot_depth)
    outgoing = pack_rows(shifted, filled, (dict_size, block_count, slot_depth, features))
    encode_received = lax.all_to_all(outgoing, "dict", split_axis=0, concat_axis=0, tiled=True)
    pre_act = jnp.einsum(
        "sbmd,bcd->sbmc", encode_received, enc_blocks, preferred_element_type=jnp.float32
    )
    pre_act = pre_act + bias_blocks[None, :, None, :]
    encode_latent = gelu_tanh(pre_act).astype(jnp.bfloat16)
    partial_value = jnp.einsum(
        "sbmc,bcd->sbmd", encode_latent, dec_blocks, preferred_element_type=jnp.float32
    ).astype(jnp.bfloat16)
    partial_value, pre_act, latent, received = (
        partial_value,
        pre_act,
        encode_latent,
        encode_received,
    )
    returned = lax.all_to_all(partial_value, "dict", split_axis=0, concat_axis=0, tiled=True)
    slot_parts = (
        returned.reshape(-1, features)[target].astype(jnp.float32).reshape(rows_here, K, features)
    )
    recon_full = dec_bias[None, :] + jnp.sum(slot_parts, axis=1)
    rebuilt = recon_full.astype(jnp.bfloat16)
    residual = ((recon_full - activations.astype(jnp.float32)) * LOSS_SCALE).astype(jnp.bfloat16)
    residual_sent = pack_rows(residual, filled, (dict_size, block_count, slot_depth, features))
    residual_held = lax.all_to_all(residual_sent, "dict", split_axis=0, concat_axis=0, tiled=True)
    upstream = jnp.einsum(
        "sbmd,bcd->sbmc", residual_held, dec_blocks, preferred_element_type=jnp.float32
    )
    latent_grad = gelu_grad(pre_act, upstream).astype(jnp.bfloat16)
    product = jnp.einsum(
        "sbmc,sbmd->dbc", latent, residual_held, preferred_element_type=jnp.float32
    )
    dec_grad = lax.psum_scatter(
        product.reshape(features // row_size * lax.axis_size("row"), local_latents),
        "row",
        scatter_dimension=0,
        tiled=True,
    ).astype(jnp.bfloat16)
    product = jnp.einsum(
        "sbmc,sbmd->dbc", latent_grad, received, preferred_element_type=jnp.float32
    )
    enc_grad = lax.psum_scatter(
        product.reshape(features // row_size * lax.axis_size("row"), local_latents),
        "row",
        scatter_dimension=0,
        tiled=True,
    ).astype(jnp.bfloat16)
    return (rebuilt, enc_grad, dec_grad)


def gelu_and_slope(values):
    inner = 0.7978845608 * (values + 0.044715 * values * values * values)
    bend = jnp.tanh(inner)
    half = 0.5 * (1.0 + bend)
    slope = half + 0.5 * values * (1.0 - bend * bend) * 0.7978845608 * (
        1.0 + 3.0 * 0.044715 * values * values
    )
    return values * half, slope


SUBS = 4


def step_kernel(
    x_ref, act_ref, bias_ref, dbias_ref, enc_ref, dec_ref,
    rebuilt_ref, enc_grad_ref, dec_grad_ref,
    held, res, enc_far, dec_far, bias_far, part, total, incoming, latent, slope,
    acc, fin, near_out, near_in, row_out, row_in,
    w_send, w_recv, x_send, x_recv, p_send, p_recv, r_send, r_recv,
    n_send, n_recv, g_send, g_recv,
):
    rows, features = act_ref.shape
    row = lax.axis_index("row")
    dict_at = lax.axis_index("dict")
    row_size = lax.axis_size("row")
    places = lax.axis_size("dict") // 2
    place = dict_at // 2
    core = dict_at % 2
    far = place * 2 + (1 - core)
    sub = rows // SUBS
    half = enc_ref.shape[0]
    slab = features // row_size
    f32, bf16 = jnp.float32, jnp.bfloat16

    def along(step):
        return (row, dict_at + 2 * step)

    def remote(src, dst, send, recv, device):
        return pltpu.make_async_remote_copy(
            src_ref=src, dst_ref=dst, send_sem=send, recv_sem=recv,
            device_id=device, device_id_type=pl.DeviceIdType.MESH,
        )

    barrier = pltpu.get_barrier_semaphore()

    def greet(device):
        pl.semaphore_signal(
            barrier, inc=1, device_id=device, device_id_type=pl.DeviceIdType.MESH
        )

    greet((row, far))
    for k in range(1, row_size):
        greet(((row + k) % row_size, dict_at))

    @pl.when(place > 0)
    def _():
        greet(along(-1))

    @pl.when(place < places - 1)
    def _():
        greet(along(1))

    inside = jnp.logical_and(place > 0, place < places - 1)

    @pl.when(inside)
    def _():
        pl.semaphore_wait(barrier, row_size + 2)

    @pl.when(jnp.logical_not(inside))
    def _():
        pl.semaphore_wait(barrier, row_size + 1)

    def part_rows(s):
        return pl.ds(pl.multiple_of(s * sub, sub), sub)

    def has_next(way):
        return jnp.logical_and(place + way >= 0, place + way < places)

    def x_copy(q, s, way, own):
        src = x_ref.at[part_rows(s)] if own else held.at[q, part_rows(s)]
        return remote(
            src, held.at[q, part_rows(s)], x_send.at[(way + 1) // 2, q, s],
            x_recv.at[q, s], along(way),
        )

    def r_copy(q, s, way):
        return remote(
            res.at[q, part_rows(s)], res.at[q, part_rows(s)],
            r_send.at[(way + 1) // 2, q, s], r_recv.at[q, s], along(way),
        )

    def p_copy(q, s, way):
        return remote(
            part.at[q, part_rows(s)], incoming.at[(way + 1) // 2, q, part_rows(s)],
            p_send.at[q, s], p_recv.at[(way + 1) // 2, q, s], along(way),
        )

    for s in range(SUBS):
        for way in (1, -1):
            @pl.when(has_next(way))
            def _():
                x_copy(place, s, way, True).start()

    weights = [
        remote(src, dst, w_send.at[i], w_recv.at[i], (row, far))
        for i, (src, dst) in enumerate(
            ((bias_ref, bias_far), (enc_ref, enc_far), (dec_ref, dec_far))
        )
    ]
    for copy in weights:
        copy.start()
    held[place] = x_ref[...]
    for copy in weights:
        copy.wait_recv()

    def forward(q):
        data = held[q, :, :features]
        active = held[q, :, features:]
        block = lax.broadcasted_iota(jnp.int32, (active.shape[1], half), 0)
        column = lax.broadcasted_iota(jnp.int32, (active.shape[1], half), 1)
        blocks = half // BS
        for h, (weight, bias, owner) in enumerate(
            ((enc_ref, bias_ref, dict_at), (enc_far, bias_far, far))
        ):
            chosen = jnp.where(block == owner * blocks + column // BS, 1.0, 0.0).astype(bf16)
            mask = jnp.dot(active, chosen, preferred_element_type=f32) > 0.5
            pre = lax.dot_general(
                data, weight[...], (((1,), (1,)), ((), ())), preferred_element_type=f32
            )
            value, bend = gelu_and_slope(pre + bias[0:1, :])
            latent[q, :, h * half : (h + 1) * half] = jnp.where(mask, value, 0.0).astype(bf16)
            slope[q, :, h * half : (h + 1) * half] = jnp.where(mask, bend, 0.0)

    def decoded(q, columns):
        return jnp.dot(
            latent[q, :, :half], dec_ref[:, columns], preferred_element_type=f32
        ) + jnp.dot(latent[q, :, half:], dec_far[:, columns], preferred_element_type=f32)

    wide = 1024

    def each_columns(body):
        @pl.loop(0, features // wide)
        def _(i):
            body(pl.ds(pl.multiple_of(i * wide, wide), wide))

    forward(place)

    def keep_total(columns):
        total[:, columns] = decoded(place, columns) + dbias_ref[:, columns]

    each_columns(keep_total)

    @pl.loop(2, 2 * places)
    def _(i):
        way = 1 - 2 * (i % 2)
        q = place - way * (i // 2)

        @pl.when(jnp.logical_and(q >= 0, q < places))
        def _():
            @pl.loop(0, SUBS)
            def _(s):
                x_copy(q, s, way, False).wait_recv()

                @pl.when(has_next(way))
                def _():
                    x_copy(q, s, way, False).start()

            forward(q)

            def keep_part(columns):
                part[q, :, columns] = decoded(q, columns).astype(bf16)

            each_columns(keep_part)

            @pl.when(jnp.logical_not(has_next(way)))
            def _():
                @pl.loop(0, SUBS)
                def _(s):
                    p_copy(q, s, -way).start()

    def finish(s):
        here = part_rows(s)
        full = total[here, :]
        rebuilt_ref[here, :] = full.astype(bf16)
        res[place, here, :] = ((full - act_ref[here, :].astype(f32)) * LOSS_SCALE).astype(bf16)
        for way in (1, -1):
            @pl.when(has_next(way))
            def _():
                r_copy(place, s, way).start()

    @pl.loop(0, 2)
    def _(turn):
        low = jnp.where(place < places // 2, 1, -1)
        way = low * (1 - 2 * turn)
        lane = (way + 1) // 2

        @pl.when(has_next(-way))
        def _():
            @pl.loop(0, places)
            def _(t):
                q = place + way * t

                @pl.when(jnp.logical_and(q >= 0, q < places))
                def _():
                    @pl.loop(0, SUBS)
                    def _(s):
                        here = part_rows(s)
                        p_copy(q, s, way).wait_recv()

                        @pl.when(t == 0)
                        def _():
                            total[here, :] += incoming[lane, q, here, :].astype(f32)

                            @pl.when(turn == 1)
                            def _():
                                finish(s)

                        @pl.when(t > 0)
                        def _():
                            part[q, here, :] = (
                                part[q, here, :].astype(f32)
                                + incoming[lane, q, here, :].astype(f32)
                            ).astype(bf16)
                            p_copy(q, s, way).start()

    def backward(q):
        for h, weight in enumerate((dec_ref, dec_far)):
            span = slice(h * half, (h + 1) * half)
            up = lax.dot_general(
                res[q], weight[...], (((1,), (1,)), ((), ())), preferred_element_type=f32
            )
            slope[q, :, span] = slope[q, :, span] * up

    backward(place)

    @pl.loop(2, 2 * places)
    def _(i):
        way = 1 - 2 * (i % 2)
        q = place - way * (i // 2)

        @pl.when(jnp.logical_and(q >= 0, q < places))
        def _():
            @pl.loop(0, SUBS)
            def _(s):
                r_copy(q, s, way).wait_recv()

                @pl.when(has_next(way))
                def _():
                    r_copy(q, s, way).start()

            backward(q)

    tile = 256

    def near_copy(g, k):
        return remote(
            near_out.at[g, k], near_in.at[g, k], n_send.at[g, k], n_recv.at[g, k], (row, far)
        )

    def row_copy(g, k):
        return remote(
            row_out.at[g, k], row_in.at[g, k], g_send.at[g, k], g_recv.at[g, k],
            ((row + k + 1) % row_size, dict_at),
        )

    for g, left in enumerate((res, held)):
        @pl.loop(0, row_size + 1)
        def _(k):
            @pl.when(k < row_size)
            def _():
                base = (row + k + 1) % row_size * slab

                @pl.loop(0, slab // tile)
                def _(i):
                    columns = pl.ds(pl.multiple_of(base + i * tile, tile), tile)
                    lefts = left[:, :, columns].reshape(places * rows, tile)
                    if g == 0:
                        rights = latent[...].reshape(places * rows, 2 * half)
                    else:
                        rights = slope[...].reshape(places * rows, 2 * half).astype(bf16)
                    product = lax.dot_general(
                        lefts, rights, (((0,), (0,)), ((), ())), preferred_element_type=f32
                    )
                    at = pl.ds(pl.multiple_of(i * tile, tile), tile)
                    acc[k % 2, at, :] = product[:, :half]
                    near_out[g, k, at, :] = product[:, half:].astype(bf16)

                near_copy(g, k).start()

            @pl.when(k > 0)
            def _():
                near_copy(g, k - 1).wait_recv()
                both = acc[(k - 1) % 2] + near_in[g, k - 1].astype(f32)

                @pl.when(k < row_size)
                def _():
                    row_out[g, k - 1] = both.astype(bf16)
                    row_copy(g, k - 1).start()

                @pl.when(k == row_size)
                def _():
                    fin[g] = both

    for g, out in enumerate((dec_grad_ref, enc_grad_ref)):
        for k in range(row_size - 1):
            row_copy(g, k).wait_recv()
        out[...] = (
            fin[g] + row_in[g, 0].astype(f32) + row_in[g, 1].astype(f32) + row_in[g, 2].astype(f32)
        ).astype(bf16)

    for copy in weights:
        copy.wait_send()

    @pl.loop(0, SUBS)
    def _(s):
        for way in (1, -1):
            @pl.when(has_next(way))
            def _():
                x_copy(place, s, way, True).wait_send()
                r_copy(place, s, way).wait_send()

                @pl.loop(0, places)
                def _(q):
                    @pl.when((q - place) * way < 0)
                    def _():
                        x_copy(q, s, way, False).wait_send()
                        r_copy(q, s, way).wait_send()

                    @pl.when((q - place) * way > 0)
                    def _():
                        p_copy(q, s, way).wait_send()

    for g in range(2):
        for k in range(row_size):
            near_copy(g, k).wait_send()
        for k in range(row_size - 1):
            row_copy(g, k).wait_send()


def fused_on_device(activations, block_ids, enc_weight, enc_bias, dec_weight, dec_bias):
    rows, features = activations.shape
    half = enc_weight.shape[0]
    places = lax.axis_size("dict") // 2
    row_size = lax.axis_size("row")
    slab = features // row_size
    f32, bf16 = jnp.float32, jnp.bfloat16
    shifted = (activations.astype(f32) - dec_bias[None, :]).astype(bf16)
    active = jnp.any(
        block_ids[:, :, None] == jnp.arange(128, dtype=jnp.int32)[None, None, :], axis=1
    ).astype(bf16)
    data = jnp.concatenate([shifted, active], axis=1)
    bias = jnp.broadcast_to(enc_bias[None, :], (8, half))
    dma = pltpu.SemaphoreType.DMA
    rebuilt, enc_grad, dec_grad = pl.pallas_call(
        step_kernel,
        out_shape=(
            jax.ShapeDtypeStruct((rows, features), bf16),
            jax.ShapeDtypeStruct((slab, half), bf16),
            jax.ShapeDtypeStruct((slab, half), bf16),
        ),
        in_specs=[pl.BlockSpec(memory_space=pltpu.VMEM)] * 6,
        out_specs=[pl.BlockSpec(memory_space=pltpu.VMEM)] * 3,
        scratch_shapes=[
            pltpu.VMEM((places, rows, features + 128), bf16),
            pltpu.VMEM((places, rows, features), bf16),
            pltpu.VMEM((half, features), bf16),
            pltpu.VMEM((half, features), bf16),
            pltpu.VMEM((8, half), f32),
            pltpu.VMEM((places, rows, features), bf16),
            pltpu.VMEM((rows, features), f32),
            pltpu.VMEM((2, places, rows, features), bf16),
            pltpu.VMEM((places, rows, 2 * half), bf16),
            pltpu.VMEM((places, rows, 2 * half), f32),
            pltpu.VMEM((2, slab, half), f32),
            pltpu.VMEM((2, slab, half), f32),
            pltpu.VMEM((2, row_size, slab, half), bf16),
            pltpu.VMEM((2, row_size, slab, half), bf16),
            pltpu.VMEM((2, row_size - 1, slab, half), bf16),
            pltpu.VMEM((2, row_size - 1, slab, half), bf16),
            dma((3,)), dma((3,)),
            dma((2, places, SUBS)), dma((places, SUBS)),
            dma((places, SUBS)), dma((2, places, SUBS)),
            dma((2, places, SUBS)), dma((places, SUBS)),
            dma((2, row_size)), dma((2, row_size)),
            dma((2, row_size - 1)), dma((2, row_size - 1)),
        ],
        compiler_params=pltpu.CompilerParams(
            collective_id=0, has_side_effects=True, vmem_limit_bytes=67043328
        ),
    )(data, activations, bias, dec_bias[None, :], enc_weight, dec_weight)
    return (rebuilt, enc_grad, dec_grad)


def solution(mesh):
    short_chain = mesh.shape["dict"] <= 8
    return jax.shard_map(
        fused_on_device if short_chain else on_device,
        mesh=mesh,
        in_specs=(
            P(("row", "dict"), None),
            P(("row", "dict"), None),
            P("dict", None),
            P("dict"),
            P("dict", None),
            P(),
        ),
        out_specs=(P(("row", "dict"), None), P("row", "dict"), P("row", "dict")),
        check_vma=False,
    )
```

```python
import jax
import jax.numpy as jnp
from jax import lax
from jax.experimental import pallas as pl
from jax.experimental.pallas import tpu as pltpu
from jax.sharding import PartitionSpec as P

BS = 128
K = 4


LOSS_SCALE = 0.03125


def gelu_tanh(values):
    return jax.nn.gelu(values, approximate=True)


def gelu_grad(pre_act, upstream):
    return jax.vjp(gelu_tanh, pre_act)[1](upstream)[0]


def slot_plan(block_ids, groups, total_blocks, slot_depth):
    rows_total = block_ids.shape[0]
    picks = block_ids.shape[1]
    per_group = rows_total // groups
    flat_ids = block_ids.reshape(groups, per_group * picks)
    onehot = (
        flat_ids[:, :, None] == jnp.arange(total_blocks, dtype=jnp.int32)[None, None, :]
    ).astype(jnp.int32)
    rank_in_block = jnp.sum((jnp.cumsum(onehot, axis=1) - 1) * onehot, axis=2)
    group_index = jnp.arange(groups, dtype=jnp.int32)[:, None]
    target = ((flat_ids * groups + group_index) * slot_depth + rank_in_block).reshape(-1)
    source_row = jnp.arange(rows_total * picks, dtype=jnp.int32) // picks
    filled = (
        jnp.full((total_blocks * groups * slot_depth,), rows_total, jnp.int32)
        .at[target]
        .set(source_row)
    )
    return (target, filled)


def pack_rows(values, filled, shape):
    padded = jnp.concatenate([values, jnp.zeros((1, values.shape[1]), values.dtype)], axis=0)
    return padded[filled].reshape(shape)


def on_device(activations, block_ids, enc_weight, enc_bias, dec_weight, dec_bias):
    rows_here, features = activations.shape
    dict_size = lax.axis_size("dict")
    row_size = lax.axis_size("row")
    local_latents = enc_weight.shape[0]
    block_count = local_latents // BS
    total_blocks = block_count * dict_size
    slot_depth = max(2, 3 * rows_here * K // (2 * total_blocks))
    enc_blocks = enc_weight.reshape(block_count, BS, features)
    dec_blocks = dec_weight.reshape(block_count, BS, features)
    bias_blocks = enc_bias.reshape(block_count, BS)
    shifted = (activations.astype(jnp.float32) - dec_bias[None, :]).astype(jnp.bfloat16)
    target, filled = slot_plan(block_ids, 1, total_blocks, slot_depth)
    outgoing = pack_rows(shifted, filled, (dict_size, block_count, slot_depth, features))
    encode_received = lax.all_to_all(outgoing, "dict", split_axis=0, concat_axis=0, tiled=True)
    pre_act = jnp.einsum(
        "sbmd,bcd->sbmc", encode_received, enc_blocks, preferred_element_type=jnp.float32
    )
    pre_act = pre_act + bias_blocks[None, :, None, :]
    encode_latent = gelu_tanh(pre_act).astype(jnp.bfloat16)
    partial_value = jnp.einsum(
        "sbmc,bcd->sbmd", encode_latent, dec_blocks, preferred_element_type=jnp.float32
    ).astype(jnp.bfloat16)
    partial_value, pre_act, latent, received = (
        partial_value,
        pre_act,
        encode_latent,
        encode_received,
    )
    returned = lax.all_to_all(partial_value, "dict", split_axis=0, concat_axis=0, tiled=True)
    slot_parts = (
        returned.reshape(-1, features)[target].astype(jnp.float32).reshape(rows_here, K, features)
    )
    recon_full = dec_bias[None, :] + jnp.sum(slot_parts, axis=1)
    rebuilt = recon_full.astype(jnp.bfloat16)
    residual = ((recon_full - activations.astype(jnp.float32)) * LOSS_SCALE).astype(jnp.bfloat16)
    residual_sent = pack_rows(residual, filled, (dict_size, block_count, slot_depth, features))
    residual_held = lax.all_to_all(residual_sent, "dict", split_axis=0, concat_axis=0, tiled=True)
    upstream = jnp.einsum(
        "sbmd,bcd->sbmc", residual_held, dec_blocks, preferred_element_type=jnp.float32
    )
    latent_grad = gelu_grad(pre_act, upstream).astype(jnp.bfloat16)
    product = jnp.einsum(
        "sbmc,sbmd->dbc", latent, residual_held, preferred_element_type=jnp.float32
    )
    dec_grad = lax.psum_scatter(
        product.reshape(features // row_size * lax.axis_size("row"), local_latents),
        "row",
        scatter_dimension=0,
        tiled=True,
    ).astype(jnp.bfloat16)
    product = jnp.einsum(
        "sbmc,sbmd->dbc", latent_grad, received, preferred_element_type=jnp.float32
    )
    enc_grad = lax.psum_scatter(
        product.reshape(features // row_size * lax.axis_size("row"), local_latents),
        "row",
        scatter_dimension=0,
        tiled=True,
    ).astype(jnp.bfloat16)
    return (rebuilt, enc_grad, dec_grad)


def gelu_and_slope(values):
    inner = 0.7978845608 * (values + 0.044715 * values * values * values)
    bend = jnp.tanh(inner)
    half = 0.5 * (1.0 + bend)
    slope = half + 0.5 * values * (1.0 - bend * bend) * 0.7978845608 * (
        1.0 + 3.0 * 0.044715 * values * values
    )
    return values * half, slope


SUBS = 4


def step_kernel(
    x_ref, act_ref, bias_ref, dbias_ref, enc_ref, dec_ref,
    rebuilt_ref, enc_grad_ref, dec_grad_ref,
    held, res, enc_far, dec_far, bias_far, part, total, incoming, latent, slope,
    acc, fin, near_out, near_in, row_out, row_in,
    w_send, w_recv, x_send, x_recv, p_send, p_recv, r_send, r_recv,
    n_send, n_recv, g_send, g_recv,
):
    rows, features = act_ref.shape
    row = lax.axis_index("row")
    dict_at = lax.axis_index("dict")
    row_size = lax.axis_size("row")
    places = lax.axis_size("dict") // 2
    place = dict_at // 2
    core = dict_at % 2
    far = place * 2 + (1 - core)
    sub = rows // SUBS
    half = enc_ref.shape[0]
    slab = features // row_size
    f32, bf16 = jnp.float32, jnp.bfloat16

    def along(step):
        return (row, dict_at + 2 * step)

    def remote(src, dst, send, recv, device):
        return pltpu.make_async_remote_copy(
            src_ref=src, dst_ref=dst, send_sem=send, recv_sem=recv,
            device_id=device, device_id_type=pl.DeviceIdType.MESH,
        )

    barrier = pltpu.get_barrier_semaphore()

    def greet(device):
        pl.semaphore_signal(
            barrier, inc=1, device_id=device, device_id_type=pl.DeviceIdType.MESH
        )

    greet((row, far))
    for k in range(1, row_size):
        greet(((row + k) % row_size, dict_at))

    @pl.when(place > 0)
    def _():
        greet(along(-1))

    @pl.when(place < places - 1)
    def _():
        greet(along(1))

    inside = jnp.logical_and(place > 0, place < places - 1)

    @pl.when(inside)
    def _():
        pl.semaphore_wait(barrier, row_size + 2)

    @pl.when(jnp.logical_not(inside))
    def _():
        pl.semaphore_wait(barrier, row_size + 1)

    def part_rows(s):
        return pl.ds(pl.multiple_of(s * sub, sub), sub)

    def has_next(way):
        return jnp.logical_and(place + way >= 0, place + way < places)

    def x_copy(q, s, way, own):
        src = x_ref.at[part_rows(s)] if own else held.at[q, part_rows(s)]
        return remote(
            src, held.at[q, part_rows(s)], x_send.at[(way + 1) // 2, q, s],
            x_recv.at[q, s], along(way),
        )

    def r_copy(q, s, way):
        return remote(
            res.at[q, part_rows(s)], res.at[q, part_rows(s)],
            r_send.at[(way + 1) // 2, q, s], r_recv.at[q, s], along(way),
        )

    def p_copy(q, s, way):
        return remote(
            part.at[q, part_rows(s)], incoming.at[(way + 1) // 2, q, part_rows(s)],
            p_send.at[q, s], p_recv.at[(way + 1) // 2, q, s], along(way),
        )

    for s in range(SUBS):
        for way in (1, -1):
            @pl.when(has_next(way))
            def _():
                x_copy(place, s, way, True).start()

    weights = [
        remote(src, dst, w_send.at[i], w_recv.at[i], (row, far))
        for i, (src, dst) in enumerate(
            ((bias_ref, bias_far), (enc_ref, enc_far), (dec_ref, dec_far))
        )
    ]
    for copy in weights:
        copy.start()
    held[place] = x_ref[...]
    for copy in weights:
        copy.wait_recv()

    def forward(q):
        data = held[q, :, :features]
        active = held[q, :, features:]
        block = lax.broadcasted_iota(jnp.int32, (active.shape[1], half), 0)
        column = lax.broadcasted_iota(jnp.int32, (active.shape[1], half), 1)
        blocks = half // BS
        for h, (weight, bias, owner) in enumerate(
            ((enc_ref, bias_ref, dict_at), (enc_far, bias_far, far))
        ):
            chosen = jnp.where(block == owner * blocks + column // BS, 1.0, 0.0).astype(bf16)
            mask = jnp.dot(active, chosen, preferred_element_type=f32) > 0.5
            pre = lax.dot_general(
                data, weight[...], (((1,), (1,)), ((), ())), preferred_element_type=f32
            )
            value, bend = gelu_and_slope(pre + bias[0:1, :])
            latent[q, :, h * half : (h + 1) * half] = jnp.where(mask, value, 0.0).astype(bf16)
            slope[q, :, h * half : (h + 1) * half] = jnp.where(mask, bend, 0.0)

    def decoded(q, columns):
        return jnp.dot(
            latent[q, :, :half], dec_ref[:, columns], preferred_element_type=f32
        ) + jnp.dot(latent[q, :, half:], dec_far[:, columns], preferred_element_type=f32)

    wide = 1024

    def each_columns(body):
        @pl.loop(0, features // wide)
        def _(i):
            body(pl.ds(pl.multiple_of(i * wide, wide), wide))

    forward(place)

    def keep_total(columns):
        total[:, columns] = decoded(place, columns) + dbias_ref[:, columns]

    each_columns(keep_total)

    @pl.loop(1, places)
    def _(distance):
        @pl.loop(0, SUBS)
        def _(s):
            for way in (1, -1):
                @pl.when(has_next(-way * distance))
                def _():
                    q = place - way * distance
                    x_copy(q, s, way, False).wait_recv()

                    @pl.when(has_next(way))
                    def _():
                        x_copy(q, s, way, False).start()

        @pl.loop(0, 2)
        def _(turn):
            way = 1 - 2 * turn
            q = place - way * distance

            @pl.when(jnp.logical_and(q >= 0, q < places))
            def _():
                forward(q)

                def keep_part(columns):
                    part[q, :, columns] = decoded(q, columns).astype(bf16)

                each_columns(keep_part)

                @pl.when(jnp.logical_not(has_next(way)))
                def _():
                    @pl.loop(0, SUBS)
                    def _(s):
                        p_copy(q, s, -way).start()

    def finish(s):
        here = part_rows(s)
        full = total[here, :]
        rebuilt_ref[here, :] = full.astype(bf16)
        res[place, here, :] = ((full - act_ref[here, :].astype(f32)) * LOSS_SCALE).astype(bf16)
        for way in (1, -1):
            @pl.when(has_next(way))
            def _():
                r_copy(place, s, way).start()

    @pl.loop(0, 2)
    def _(turn):
        low = jnp.where(place < places // 2, 1, -1)
        way = low * (1 - 2 * turn)
        lane = (way + 1) // 2

        @pl.when(has_next(-way))
        def _():
            @pl.loop(0, places)
            def _(t):
                q = place + way * t

                @pl.when(jnp.logical_and(q >= 0, q < places))
                def _():
                    @pl.loop(0, SUBS)
                    def _(s):
                        here = part_rows(s)
                        p_copy(q, s, way).wait_recv()

                        @pl.when(t == 0)
                        def _():
                            total[here, :] += incoming[lane, q, here, :].astype(f32)

                            @pl.when(turn == 1)
                            def _():
                                finish(s)

                        @pl.when(t > 0)
                        def _():
                            part[q, here, :] = (
                                part[q, here, :].astype(f32)
                                + incoming[lane, q, here, :].astype(f32)
                            ).astype(bf16)
                            p_copy(q, s, way).start()

    def backward(q):
        for h, weight in enumerate((dec_ref, dec_far)):
            span = slice(h * half, (h + 1) * half)
            up = lax.dot_general(
                res[q], weight[...], (((1,), (1,)), ((), ())), preferred_element_type=f32
            )
            slope[q, :, span] = slope[q, :, span] * up

    backward(place)

    def take_residual(q, s):
        way = jnp.where(q < place, 1, -1)
        r_copy(q, s, way).wait_recv()

        @pl.when(has_next(way))
        def _():
            r_copy(q, s, way).start()

    low = place < places // 2
    first = jnp.where(low, place + 1, place - 1)
    second = jnp.where(low, 2 - 2 * place, 7 - 2 * place)
    third = jnp.where(low, 3, 0)

    @pl.loop(0, SUBS)
    def _(s):
        take_residual(first, s)

    backward(first)

    @pl.loop(0, SUBS)
    def _(s):
        take_residual(second, s)
        take_residual(third, s)

    @pl.loop(0, 2)
    def _(turn):
        backward(jnp.where(turn == 0, second, third))

    tile = 256

    def near_copy(g, k):
        return remote(
            near_out.at[g, k], near_in.at[g, k], n_send.at[g, k], n_recv.at[g, k], (row, far)
        )

    def row_copy(g, k):
        return remote(
            row_out.at[g, k], row_in.at[g, k], g_send.at[g, k], g_recv.at[g, k],
            ((row + k + 1) % row_size, dict_at),
        )

    for g, left in enumerate((res, held)):
        @pl.loop(0, row_size + 1)
        def _(k):
            @pl.when(k < row_size)
            def _():
                base = (row + k + 1) % row_size * slab

                @pl.loop(0, slab // tile)
                def _(i):
                    columns = pl.ds(pl.multiple_of(base + i * tile, tile), tile)
                    lefts = left[:, :, columns].reshape(places * rows, tile)
                    if g == 0:
                        rights = latent[...].reshape(places * rows, 2 * half)
                    else:
                        rights = slope[...].reshape(places * rows, 2 * half).astype(bf16)
                    product = lax.dot_general(
                        lefts, rights, (((0,), (0,)), ((), ())), preferred_element_type=f32
                    )
                    at = pl.ds(pl.multiple_of(i * tile, tile), tile)
                    acc[k % 2, at, :] = product[:, :half]
                    near_out[g, k, at, :] = product[:, half:].astype(bf16)

                near_copy(g, k).start()

            @pl.when(k > 0)
            def _():
                near_copy(g, k - 1).wait_recv()
                both = acc[(k - 1) % 2] + near_in[g, k - 1].astype(f32)

                @pl.when(k < row_size)
                def _():
                    row_out[g, k - 1] = both.astype(bf16)
                    row_copy(g, k - 1).start()

                @pl.when(k == row_size)
                def _():
                    fin[g] = both

    for g, out in enumerate((dec_grad_ref, enc_grad_ref)):
        for k in range(row_size - 1):
            row_copy(g, k).wait_recv()
        out[...] = (
            fin[g] + row_in[g, 0].astype(f32) + row_in[g, 1].astype(f32) + row_in[g, 2].astype(f32)
        ).astype(bf16)

    for copy in weights:
        copy.wait_send()

    @pl.loop(0, SUBS)
    def _(s):
        for way in (1, -1):
            @pl.when(has_next(way))
            def _():
                x_copy(place, s, way, True).wait_send()
                r_copy(place, s, way).wait_send()

                @pl.loop(0, places)
                def _(q):
                    @pl.when((q - place) * way < 0)
                    def _():
                        x_copy(q, s, way, False).wait_send()
                        r_copy(q, s, way).wait_send()

                    @pl.when((q - place) * way > 0)
                    def _():
                        p_copy(q, s, way).wait_send()

    for g in range(2):
        for k in range(row_size):
            near_copy(g, k).wait_send()
        for k in range(row_size - 1):
            row_copy(g, k).wait_send()


def fused_on_device(activations, block_ids, enc_weight, enc_bias, dec_weight, dec_bias):
    rows, features = activations.shape
    half = enc_weight.shape[0]
    places = lax.axis_size("dict") // 2
    row_size = lax.axis_size("row")
    slab = features // row_size
    f32, bf16 = jnp.float32, jnp.bfloat16
    shifted = (activations.astype(f32) - dec_bias[None, :]).astype(bf16)
    active = jnp.any(
        block_ids[:, :, None] == jnp.arange(128, dtype=jnp.int32)[None, None, :], axis=1
    ).astype(bf16)
    data = jnp.concatenate([shifted, active], axis=1)
    bias = jnp.broadcast_to(enc_bias[None, :], (8, half))
    dma = pltpu.SemaphoreType.DMA
    rebuilt, enc_grad, dec_grad = pl.pallas_call(
        step_kernel,
        out_shape=(
            jax.ShapeDtypeStruct((rows, features), bf16),
            jax.ShapeDtypeStruct((slab, half), bf16),
            jax.ShapeDtypeStruct((slab, half), bf16),
        ),
        in_specs=[pl.BlockSpec(memory_space=pltpu.VMEM)] * 6,
        out_specs=[pl.BlockSpec(memory_space=pltpu.VMEM)] * 3,
        scratch_shapes=[
            pltpu.VMEM((places, rows, features + 128), bf16),
            pltpu.VMEM((places, rows, features), bf16),
            pltpu.VMEM((half, features), bf16),
            pltpu.VMEM((half, features), bf16),
            pltpu.VMEM((8, half), f32),
            pltpu.VMEM((places, rows, features), bf16),
            pltpu.VMEM((rows, features), f32),
            pltpu.VMEM((2, places, rows, features), bf16),
            pltpu.VMEM((places, rows, 2 * half), bf16),
            pltpu.VMEM((places, rows, 2 * half), f32),
            pltpu.VMEM((2, slab, half), f32),
            pltpu.VMEM((2, slab, half), f32),
            pltpu.VMEM((2, row_size, slab, half), bf16),
            pltpu.VMEM((2, row_size, slab, half), bf16),
            pltpu.VMEM((2, row_size - 1, slab, half), bf16),
            pltpu.VMEM((2, row_size - 1, slab, half), bf16),
            dma((3,)), dma((3,)),
            dma((2, places, SUBS)), dma((places, SUBS)),
            dma((places, SUBS)), dma((2, places, SUBS)),
            dma((2, places, SUBS)), dma((places, SUBS)),
            dma((2, row_size)), dma((2, row_size)),
            dma((2, row_size - 1)), dma((2, row_size - 1)),
        ],
        compiler_params=pltpu.CompilerParams(
            collective_id=0, has_side_effects=True, vmem_limit_bytes=67043328
        ),
    )(data, activations, bias, dec_bias[None, :], enc_weight, dec_weight)
    return (rebuilt, enc_grad, dec_grad)


def solution(mesh):
    short_chain = mesh.shape["dict"] == 8 and mesh.shape["row"] == 4
    return jax.shard_map(
        fused_on_device if short_chain else on_device,
        mesh=mesh,
        in_specs=(
            P(("row", "dict"), None),
            P(("row", "dict"), None),
            P("dict", None),
            P("dict"),
            P("dict", None),
            P(),
        ),
        out_specs=(P(("row", "dict"), None), P("row", "dict"), P("row", "dict")),
        check_vma=False,
    )
```

```python
import jax
import jax.numpy as jnp
from jax import lax
from jax.experimental import pallas as pl
from jax.experimental.pallas import tpu as pltpu
from jax.sharding import PartitionSpec as P

BS = 128
K = 4


LOSS_SCALE = 0.03125


def gelu_tanh(values):
    return jax.nn.gelu(values, approximate=True)


def gelu_grad(pre_act, upstream):
    return jax.vjp(gelu_tanh, pre_act)[1](upstream)[0]


def slot_plan(block_ids, groups, total_blocks, slot_depth):
    rows_total = block_ids.shape[0]
    picks = block_ids.shape[1]
    per_group = rows_total // groups
    flat_ids = block_ids.reshape(groups, per_group * picks)
    onehot = (
        flat_ids[:, :, None] == jnp.arange(total_blocks, dtype=jnp.int32)[None, None, :]
    ).astype(jnp.int32)
    rank_in_block = jnp.sum((jnp.cumsum(onehot, axis=1) - 1) * onehot, axis=2)
    group_index = jnp.arange(groups, dtype=jnp.int32)[:, None]
    target = ((flat_ids * groups + group_index) * slot_depth + rank_in_block).reshape(-1)
    source_row = jnp.arange(rows_total * picks, dtype=jnp.int32) // picks
    filled = (
        jnp.full((total_blocks * groups * slot_depth,), rows_total, jnp.int32)
        .at[target]
        .set(source_row)
    )
    return (target, filled)


def pack_rows(values, filled, shape):
    padded = jnp.concatenate([values, jnp.zeros((1, values.shape[1]), values.dtype)], axis=0)
    return padded[filled].reshape(shape)


def on_device(activations, block_ids, enc_weight, enc_bias, dec_weight, dec_bias):
    rows_here, features = activations.shape
    dict_size = lax.axis_size("dict")
    row_size = lax.axis_size("row")
    local_latents = enc_weight.shape[0]
    block_count = local_latents // BS
    total_blocks = block_count * dict_size
    slot_depth = max(2, 3 * rows_here * K // (2 * total_blocks))
    enc_blocks = enc_weight.reshape(block_count, BS, features)
    dec_blocks = dec_weight.reshape(block_count, BS, features)
    bias_blocks = enc_bias.reshape(block_count, BS)
    shifted = (activations.astype(jnp.float32) - dec_bias[None, :]).astype(jnp.bfloat16)
    target, filled = slot_plan(block_ids, 1, total_blocks, slot_depth)
    outgoing = pack_rows(shifted, filled, (dict_size, block_count, slot_depth, features))
    encode_received = lax.all_to_all(outgoing, "dict", split_axis=0, concat_axis=0, tiled=True)
    pre_act = jnp.einsum(
        "sbmd,bcd->sbmc", encode_received, enc_blocks, preferred_element_type=jnp.float32
    )
    pre_act = pre_act + bias_blocks[None, :, None, :]
    encode_latent = gelu_tanh(pre_act).astype(jnp.bfloat16)
    partial_value = jnp.einsum(
        "sbmc,bcd->sbmd", encode_latent, dec_blocks, preferred_element_type=jnp.float32
    ).astype(jnp.bfloat16)
    partial_value, pre_act, latent, received = (
        partial_value,
        pre_act,
        encode_latent,
        encode_received,
    )
    returned = lax.all_to_all(partial_value, "dict", split_axis=0, concat_axis=0, tiled=True)
    slot_parts = (
        returned.reshape(-1, features)[target].astype(jnp.float32).reshape(rows_here, K, features)
    )
    recon_full = dec_bias[None, :] + jnp.sum(slot_parts, axis=1)
    rebuilt = recon_full.astype(jnp.bfloat16)
    residual = ((recon_full - activations.astype(jnp.float32)) * LOSS_SCALE).astype(jnp.bfloat16)
    residual_sent = pack_rows(residual, filled, (dict_size, block_count, slot_depth, features))
    residual_held = lax.all_to_all(residual_sent, "dict", split_axis=0, concat_axis=0, tiled=True)
    upstream = jnp.einsum(
        "sbmd,bcd->sbmc", residual_held, dec_blocks, preferred_element_type=jnp.float32
    )
    latent_grad = gelu_grad(pre_act, upstream).astype(jnp.bfloat16)
    product = jnp.einsum(
        "sbmc,sbmd->dbc", latent, residual_held, preferred_element_type=jnp.float32
    )
    dec_grad = lax.psum_scatter(
        product.reshape(features // row_size * lax.axis_size("row"), local_latents),
        "row",
        scatter_dimension=0,
        tiled=True,
    ).astype(jnp.bfloat16)
    product = jnp.einsum(
        "sbmc,sbmd->dbc", latent_grad, received, preferred_element_type=jnp.float32
    )
    enc_grad = lax.psum_scatter(
        product.reshape(features // row_size * lax.axis_size("row"), local_latents),
        "row",
        scatter_dimension=0,
        tiled=True,
    ).astype(jnp.bfloat16)
    return (rebuilt, enc_grad, dec_grad)


def gelu_and_slope(values):
    inner = 0.7978845608 * (values + 0.044715 * values * values * values)
    bend = jnp.tanh(inner)
    half = 0.5 * (1.0 + bend)
    slope = half + 0.5 * values * (1.0 - bend * bend) * 0.7978845608 * (
        1.0 + 3.0 * 0.044715 * values * values
    )
    return values * half, slope


SUBS = 4


def step_kernel(
    x_ref, act_ref, bias_ref, dbias_ref, enc_ref, dec_ref,
    rebuilt_ref, enc_grad_ref, dec_grad_ref,
    held, res, enc_far, dec_far, bias_far, part, total, incoming, latent, slope,
    acc, fin, near_out, near_in, row_out, row_in,
    w_send, w_recv, x_send, x_recv, p_send, p_recv, r_send, r_recv,
    n_send, n_recv, g_send, g_recv,
):
    rows, features = act_ref.shape
    row = lax.axis_index("row")
    dict_at = lax.axis_index("dict")
    row_size = lax.axis_size("row")
    places = lax.axis_size("dict") // 2
    place = dict_at // 2
    core = dict_at % 2
    far = place * 2 + (1 - core)
    sub = rows // SUBS
    half = enc_ref.shape[0]
    slab = features // row_size
    f32, bf16 = jnp.float32, jnp.bfloat16

    def along(step):
        return (row, dict_at + 2 * step)

    def remote(src, dst, send, recv, device):
        return pltpu.make_async_remote_copy(
            src_ref=src, dst_ref=dst, send_sem=send, recv_sem=recv,
            device_id=device, device_id_type=pl.DeviceIdType.MESH,
        )

    barrier = pltpu.get_barrier_semaphore()

    def greet(device):
        pl.semaphore_signal(
            barrier, inc=1, device_id=device, device_id_type=pl.DeviceIdType.MESH
        )

    greet((row, far))
    for k in range(1, row_size):
        greet(((row + k) % row_size, dict_at))

    @pl.when(place > 0)
    def _():
        greet(along(-1))

    @pl.when(place < places - 1)
    def _():
        greet(along(1))

    inside = jnp.logical_and(place > 0, place < places - 1)

    @pl.when(inside)
    def _():
        pl.semaphore_wait(barrier, row_size + 2)

    @pl.when(jnp.logical_not(inside))
    def _():
        pl.semaphore_wait(barrier, row_size + 1)

    def part_rows(s):
        return pl.ds(pl.multiple_of(s * sub, sub), sub)

    def has_next(way):
        return jnp.logical_and(place + way >= 0, place + way < places)

    def x_copy(q, s, way, own):
        src = x_ref.at[part_rows(s)] if own else held.at[q, part_rows(s)]
        return remote(
            src, held.at[q, part_rows(s)], x_send.at[(way + 1) // 2, q, s],
            x_recv.at[q, s], along(way),
        )

    def r_copy(q, s, way):
        return remote(
            res.at[q, part_rows(s)], res.at[q, part_rows(s)],
            r_send.at[(way + 1) // 2, q, s], r_recv.at[q, s], along(way),
        )

    def p_copy(q, s, way):
        return remote(
            part.at[q, part_rows(s)], incoming.at[(way + 1) // 2, q, part_rows(s)],
            p_send.at[q, s], p_recv.at[(way + 1) // 2, q, s], along(way),
        )

    for s in range(SUBS):
        for way in (1, -1):
            @pl.when(has_next(way))
            def _():
                x_copy(place, s, way, True).start()

    weights = [
        remote(src, dst, w_send.at[i], w_recv.at[i], (row, far))
        for i, (src, dst) in enumerate(
            ((bias_ref, bias_far), (enc_ref, enc_far), (dec_ref, dec_far))
        )
    ]
    for copy in weights:
        copy.start()
    held[place] = x_ref[...]
    for copy in weights:
        copy.wait_recv()

    def forward(q):
        data = held[q, :, :features]
        active = held[q, :, features:]
        block = lax.broadcasted_iota(jnp.int32, (active.shape[1], half), 0)
        column = lax.broadcasted_iota(jnp.int32, (active.shape[1], half), 1)
        blocks = half // BS
        for h, (weight, bias, owner) in enumerate(
            ((enc_ref, bias_ref, dict_at), (enc_far, bias_far, far))
        ):
            chosen = jnp.where(block == owner * blocks + column // BS, 1.0, 0.0).astype(bf16)
            mask = jnp.dot(active, chosen, preferred_element_type=f32) > 0.5
            pre = lax.dot_general(
                data, weight[...], (((1,), (1,)), ((), ())), preferred_element_type=f32
            )
            value, bend = gelu_and_slope(pre + bias[0:1, :])
            latent[q, :, h * half : (h + 1) * half] = jnp.where(mask, value, 0.0).astype(bf16)
            slope[q, :, h * half : (h + 1) * half] = jnp.where(mask, bend, 0.0)

    def decoded(q, columns):
        return jnp.dot(
            latent[q, :, :half], dec_ref[:, columns], preferred_element_type=f32
        ) + jnp.dot(latent[q, :, half:], dec_far[:, columns], preferred_element_type=f32)

    wide = 1024

    def each_columns(body):
        @pl.loop(0, features // wide)
        def _(i):
            body(pl.ds(pl.multiple_of(i * wide, wide), wide))

    forward(place)

    def keep_total(columns):
        total[:, columns] = decoded(place, columns) + dbias_ref[:, columns]

    each_columns(keep_total)

    @pl.loop(1, places)
    def _(distance):
        @pl.loop(0, SUBS)
        def _(s):
            for way in (1, -1):
                @pl.when(has_next(-way * distance))
                def _():
                    q = place - way * distance
                    x_copy(q, s, way, False).wait_recv()

                    @pl.when(has_next(way))
                    def _():
                        x_copy(q, s, way, False).start()

        @pl.loop(0, 2)
        def _(turn):
            way = 1 - 2 * turn
            q = place - way * distance

            @pl.when(jnp.logical_and(q >= 0, q < places))
            def _():
                forward(q)

                def keep_part(columns):
                    part[q, :, columns] = decoded(q, columns).astype(bf16)

                each_columns(keep_part)

                @pl.when(jnp.logical_not(has_next(way)))
                def _():
                    @pl.loop(0, SUBS)
                    def _(s):
                        p_copy(q, s, -way).start()

    def finish(s):
        here = part_rows(s)
        full = total[here, :]
        rebuilt_ref[here, :] = full.astype(bf16)
        res[place, here, :] = ((full - act_ref[here, :].astype(f32)) * LOSS_SCALE).astype(bf16)
        for way in (1, -1):
            @pl.when(has_next(way))
            def _():
                r_copy(place, s, way).start()

    ahead = jnp.where(place < places // 2, 1, -1)

    def add_own(s, way):
        here = part_rows(s)
        p_copy(place, s, way).wait_recv()
        total[here, :] += incoming[(way + 1) // 2, place, here, :].astype(f32)

    def pass_on(q, s, way):
        here = part_rows(s)
        p_copy(q, s, way).wait_recv()
        part[q, here, :] = (
            part[q, here, :].astype(f32) + incoming[(way + 1) // 2, q, here, :].astype(f32)
        ).astype(bf16)
        p_copy(q, s, way).start()

    @pl.when(inside)
    def _():
        @pl.loop(0, SUBS)
        def _(s):
            add_own(s, ahead)

        @pl.loop(0, SUBS)
        def _(s):
            pass_on(place + ahead, s, ahead)

    @pl.loop(0, SUBS)
    def _(s):
        add_own(s, -ahead)
        finish(s)

    @pl.when(inside)
    def _():
        @pl.loop(0, SUBS)
        def _(s):
            pass_on(place + 2 * ahead, s, ahead)
            pass_on(place - ahead, s, -ahead)

    def backward(q):
        for h, weight in enumerate((dec_ref, dec_far)):
            span = slice(h * half, (h + 1) * half)
            up = lax.dot_general(
                res[q], weight[...], (((1,), (1,)), ((), ())), preferred_element_type=f32
            )
            slope[q, :, span] = slope[q, :, span] * up

    backward(place)

    def take_residual(q, s):
        way = jnp.where(q < place, 1, -1)
        r_copy(q, s, way).wait_recv()

        @pl.when(has_next(way))
        def _():
            r_copy(q, s, way).start()

    low = place < places // 2
    first = jnp.where(low, place + 1, place - 1)
    second = jnp.where(low, 2 - 2 * place, 7 - 2 * place)
    third = jnp.where(low, 3, 0)

    @pl.loop(0, SUBS)
    def _(s):
        take_residual(first, s)

    backward(first)

    @pl.loop(0, SUBS)
    def _(s):
        take_residual(second, s)
        take_residual(third, s)

    @pl.loop(0, 2)
    def _(turn):
        backward(jnp.where(turn == 0, second, third))

    tile = 256

    def near_copy(g, k):
        return remote(
            near_out.at[g, k], near_in.at[g, k], n_send.at[g, k], n_recv.at[g, k], (row, far)
        )

    def row_copy(g, k):
        return remote(
            row_out.at[g, k], row_in.at[g, k], g_send.at[g, k], g_recv.at[g, k],
            ((row + k + 1) % row_size, dict_at),
        )

    for g, left in enumerate((res, held)):
        @pl.loop(0, row_size + 1)
        def _(k):
            @pl.when(k < row_size)
            def _():
                base = (row + k + 1) % row_size * slab

                @pl.loop(0, slab // tile)
                def _(i):
                    columns = pl.ds(pl.multiple_of(base + i * tile, tile), tile)
                    lefts = left[:, :, columns].reshape(places * rows, tile)
                    if g == 0:
                        rights = latent[...].reshape(places * rows, 2 * half)
                    else:
                        rights = slope[...].reshape(places * rows, 2 * half).astype(bf16)
                    product = lax.dot_general(
                        lefts, rights, (((0,), (0,)), ((), ())), preferred_element_type=f32
                    )
                    at = pl.ds(pl.multiple_of(i * tile, tile), tile)
                    acc[k % 2, at, :] = product[:, :half]
                    near_out[g, k, at, :] = product[:, half:].astype(bf16)

                near_copy(g, k).start()

            @pl.when(k > 0)
            def _():
                near_copy(g, k - 1).wait_recv()
                both = acc[(k - 1) % 2] + near_in[g, k - 1].astype(f32)

                @pl.when(k < row_size)
                def _():
                    row_out[g, k - 1] = both.astype(bf16)
                    row_copy(g, k - 1).start()

                @pl.when(k == row_size)
                def _():
                    fin[g] = both

    for g, out in enumerate((dec_grad_ref, enc_grad_ref)):
        for k in range(row_size - 1):
            row_copy(g, k).wait_recv()
        out[...] = (
            fin[g] + row_in[g, 0].astype(f32) + row_in[g, 1].astype(f32) + row_in[g, 2].astype(f32)
        ).astype(bf16)

    for copy in weights:
        copy.wait_send()

    @pl.loop(0, SUBS)
    def _(s):
        for way in (1, -1):
            @pl.when(has_next(way))
            def _():
                x_copy(place, s, way, True).wait_send()
                r_copy(place, s, way).wait_send()

                @pl.loop(0, places)
                def _(q):
                    @pl.when((q - place) * way < 0)
                    def _():
                        x_copy(q, s, way, False).wait_send()
                        r_copy(q, s, way).wait_send()

                    @pl.when((q - place) * way > 0)
                    def _():
                        p_copy(q, s, way).wait_send()

    for g in range(2):
        for k in range(row_size):
            near_copy(g, k).wait_send()
        for k in range(row_size - 1):
            row_copy(g, k).wait_send()


def fused_on_device(activations, block_ids, enc_weight, enc_bias, dec_weight, dec_bias):
    rows, features = activations.shape
    half = enc_weight.shape[0]
    places = lax.axis_size("dict") // 2
    row_size = lax.axis_size("row")
    slab = features // row_size
    f32, bf16 = jnp.float32, jnp.bfloat16
    shifted = (activations.astype(f32) - dec_bias[None, :]).astype(bf16)
    active = jnp.any(
        block_ids[:, :, None] == jnp.arange(128, dtype=jnp.int32)[None, None, :], axis=1
    ).astype(bf16)
    data = jnp.concatenate([shifted, active], axis=1)
    bias = jnp.broadcast_to(enc_bias[None, :], (8, half))
    dma = pltpu.SemaphoreType.DMA
    rebuilt, enc_grad, dec_grad = pl.pallas_call(
        step_kernel,
        out_shape=(
            jax.ShapeDtypeStruct((rows, features), bf16),
            jax.ShapeDtypeStruct((slab, half), bf16),
            jax.ShapeDtypeStruct((slab, half), bf16),
        ),
        in_specs=[pl.BlockSpec(memory_space=pltpu.VMEM)] * 6,
        out_specs=[pl.BlockSpec(memory_space=pltpu.VMEM)] * 3,
        scratch_shapes=[
            pltpu.VMEM((places, rows, features + 128), bf16),
            pltpu.VMEM((places, rows, features), bf16),
            pltpu.VMEM((half, features), bf16),
            pltpu.VMEM((half, features), bf16),
            pltpu.VMEM((8, half), f32),
            pltpu.VMEM((places, rows, features), bf16),
            pltpu.VMEM((rows, features), f32),
            pltpu.VMEM((2, places, rows, features), bf16),
            pltpu.VMEM((places, rows, 2 * half), bf16),
            pltpu.VMEM((places, rows, 2 * half), f32),
            pltpu.VMEM((2, slab, half), f32),
            pltpu.VMEM((2, slab, half), f32),
            pltpu.VMEM((2, row_size, slab, half), bf16),
            pltpu.VMEM((2, row_size, slab, half), bf16),
            pltpu.VMEM((2, row_size - 1, slab, half), bf16),
            pltpu.VMEM((2, row_size - 1, slab, half), bf16),
            dma((3,)), dma((3,)),
            dma((2, places, SUBS)), dma((places, SUBS)),
            dma((places, SUBS)), dma((2, places, SUBS)),
            dma((2, places, SUBS)), dma((places, SUBS)),
            dma((2, row_size)), dma((2, row_size)),
            dma((2, row_size - 1)), dma((2, row_size - 1)),
        ],
        compiler_params=pltpu.CompilerParams(
            collective_id=0, has_side_effects=True, vmem_limit_bytes=67043328
        ),
    )(data, activations, bias, dec_bias[None, :], enc_weight, dec_weight)
    return (rebuilt, enc_grad, dec_grad)


def solution(mesh):
    short_chain = mesh.shape["dict"] == 8 and mesh.shape["row"] == 4
    return jax.shard_map(
        fused_on_device if short_chain else on_device,
        mesh=mesh,
        in_specs=(
            P(("row", "dict"), None),
            P(("row", "dict"), None),
            P("dict", None),
            P("dict"),
            P("dict", None),
            P(),
        ),
        out_specs=(P(("row", "dict"), None), P("row", "dict"), P("row", "dict")),
        check_vma=False,
    )
```

```python
import jax
import jax.numpy as jnp
from jax import lax
from jax.experimental import pallas as pl
from jax.experimental.pallas import tpu as pltpu
from jax.sharding import PartitionSpec as P

BS = 128
K = 4


LOSS_SCALE = 0.03125


def gelu_tanh(values):
    return jax.nn.gelu(values, approximate=True)


def gelu_grad(pre_act, upstream):
    return jax.vjp(gelu_tanh, pre_act)[1](upstream)[0]


def slot_plan(block_ids, groups, total_blocks, slot_depth):
    rows_total = block_ids.shape[0]
    picks = block_ids.shape[1]
    per_group = rows_total // groups
    flat_ids = block_ids.reshape(groups, per_group * picks)
    onehot = (
        flat_ids[:, :, None] == jnp.arange(total_blocks, dtype=jnp.int32)[None, None, :]
    ).astype(jnp.int32)
    rank_in_block = jnp.sum((jnp.cumsum(onehot, axis=1) - 1) * onehot, axis=2)
    group_index = jnp.arange(groups, dtype=jnp.int32)[:, None]
    target = ((flat_ids * groups + group_index) * slot_depth + rank_in_block).reshape(-1)
    source_row = jnp.arange(rows_total * picks, dtype=jnp.int32) // picks
    filled = (
        jnp.full((total_blocks * groups * slot_depth,), rows_total, jnp.int32)
        .at[target]
        .set(source_row)
    )
    return (target, filled)


def pack_rows(values, filled, shape):
    padded = jnp.concatenate([values, jnp.zeros((1, values.shape[1]), values.dtype)], axis=0)
    return padded[filled].reshape(shape)


def on_device(activations, block_ids, enc_weight, enc_bias, dec_weight, dec_bias):
    rows_here, features = activations.shape
    dict_size = lax.axis_size("dict")
    row_size = lax.axis_size("row")
    local_latents = enc_weight.shape[0]
    block_count = local_latents // BS
    total_blocks = block_count * dict_size
    slot_depth = max(2, 3 * rows_here * K // (2 * total_blocks))
    enc_blocks = enc_weight.reshape(block_count, BS, features)
    dec_blocks = dec_weight.reshape(block_count, BS, features)
    bias_blocks = enc_bias.reshape(block_count, BS)
    shifted = (activations.astype(jnp.float32) - dec_bias[None, :]).astype(jnp.bfloat16)
    target, filled = slot_plan(block_ids, 1, total_blocks, slot_depth)
    outgoing = pack_rows(shifted, filled, (dict_size, block_count, slot_depth, features))
    encode_received = lax.all_to_all(outgoing, "dict", split_axis=0, concat_axis=0, tiled=True)
    pre_act = jnp.einsum(
        "sbmd,bcd->sbmc", encode_received, enc_blocks, preferred_element_type=jnp.float32
    )
    pre_act = pre_act + bias_blocks[None, :, None, :]
    encode_latent = gelu_tanh(pre_act).astype(jnp.bfloat16)
    partial_value = jnp.einsum(
        "sbmc,bcd->sbmd", encode_latent, dec_blocks, preferred_element_type=jnp.float32
    ).astype(jnp.bfloat16)
    partial_value, pre_act, latent, received = (
        partial_value,
        pre_act,
        encode_latent,
        encode_received,
    )
    returned = lax.all_to_all(partial_value, "dict", split_axis=0, concat_axis=0, tiled=True)
    slot_parts = (
        returned.reshape(-1, features)[target].astype(jnp.float32).reshape(rows_here, K, features)
    )
    recon_full = dec_bias[None, :] + jnp.sum(slot_parts, axis=1)
    rebuilt = recon_full.astype(jnp.bfloat16)
    residual = ((recon_full - activations.astype(jnp.float32)) * LOSS_SCALE).astype(jnp.bfloat16)
    residual_sent = pack_rows(residual, filled, (dict_size, block_count, slot_depth, features))
    residual_held = lax.all_to_all(residual_sent, "dict", split_axis=0, concat_axis=0, tiled=True)
    upstream = jnp.einsum(
        "sbmd,bcd->sbmc", residual_held, dec_blocks, preferred_element_type=jnp.float32
    )
    latent_grad = gelu_grad(pre_act, upstream).astype(jnp.bfloat16)
    product = jnp.einsum(
        "sbmc,sbmd->dbc", latent, residual_held, preferred_element_type=jnp.float32
    )
    dec_grad = lax.psum_scatter(
        product.reshape(features // row_size * lax.axis_size("row"), local_latents),
        "row",
        scatter_dimension=0,
        tiled=True,
    ).astype(jnp.bfloat16)
    product = jnp.einsum(
        "sbmc,sbmd->dbc", latent_grad, received, preferred_element_type=jnp.float32
    )
    enc_grad = lax.psum_scatter(
        product.reshape(features // row_size * lax.axis_size("row"), local_latents),
        "row",
        scatter_dimension=0,
        tiled=True,
    ).astype(jnp.bfloat16)
    return (rebuilt, enc_grad, dec_grad)


def gelu_and_slope(values):
    inner = 0.7978845608 * (values + 0.044715 * values * values * values)
    bend = jnp.tanh(inner)
    half = 0.5 * (1.0 + bend)
    slope = half + 0.5 * values * (1.0 - bend * bend) * 0.7978845608 * (
        1.0 + 3.0 * 0.044715 * values * values
    )
    return values * half, slope


SUBS = 4


def step_kernel(
    x_ref, act_ref, bias_ref, dbias_ref, enc_ref, dec_ref,
    rebuilt_ref, enc_grad_ref, dec_grad_ref,
    held, res, enc_far, dec_far, bias_far, part, total, incoming, latent, slope,
    acc, fin, near_out, near_in, row_out, row_in,
    w_send, w_recv, x_send, x_recv, p_send, p_recv, r_send, r_recv,
    n_send, n_recv, g_send, g_recv,
):
    rows, features = act_ref.shape
    row = lax.axis_index("row")
    dict_at = lax.axis_index("dict")
    row_size = lax.axis_size("row")
    places = lax.axis_size("dict") // 2
    place = dict_at // 2
    core = dict_at % 2
    far = place * 2 + (1 - core)
    sub = rows // SUBS
    half = enc_ref.shape[0]
    slab = features // row_size
    f32, bf16 = jnp.float32, jnp.bfloat16

    def along(step):
        return (row, dict_at + 2 * step)

    def remote(src, dst, send, recv, device):
        return pltpu.make_async_remote_copy(
            src_ref=src, dst_ref=dst, send_sem=send, recv_sem=recv,
            device_id=device, device_id_type=pl.DeviceIdType.MESH,
        )

    barrier = pltpu.get_barrier_semaphore()

    def greet(device):
        pl.semaphore_signal(
            barrier, inc=1, device_id=device, device_id_type=pl.DeviceIdType.MESH
        )

    greet((row, far))
    for k in range(1, row_size):
        greet(((row + k) % row_size, dict_at))

    @pl.when(place > 0)
    def _():
        greet(along(-1))

    @pl.when(place < places - 1)
    def _():
        greet(along(1))

    inside = jnp.logical_and(place > 0, place < places - 1)

    @pl.when(inside)
    def _():
        pl.semaphore_wait(barrier, row_size + 2)

    @pl.when(jnp.logical_not(inside))
    def _():
        pl.semaphore_wait(barrier, row_size + 1)

    def part_rows(s):
        return pl.ds(pl.multiple_of(s * sub, sub), sub)

    def has_next(way):
        return jnp.logical_and(place + way >= 0, place + way < places)

    def x_copy(q, s, way, own):
        src = x_ref.at[part_rows(s)] if own else held.at[q, part_rows(s)]
        return remote(
            src, held.at[q, part_rows(s)], x_send.at[(way + 1) // 2, q, s],
            x_recv.at[q, s], along(way),
        )

    def r_copy(q, s, way):
        return remote(
            res.at[q, part_rows(s)], res.at[q, part_rows(s)],
            r_send.at[(way + 1) // 2, q, s], r_recv.at[q, s], along(way),
        )

    def p_copy(q, s, way):
        return remote(
            part.at[q, part_rows(s)], incoming.at[(way + 1) // 2, q, part_rows(s)],
            p_send.at[q, s], p_recv.at[(way + 1) // 2, q, s], along(way),
        )

    for s in range(SUBS):
        for way in (1, -1):
            @pl.when(has_next(way))
            def _():
                x_copy(place, s, way, True).start()

    weights = [
        remote(src, dst, w_send.at[i], w_recv.at[i], (row, far))
        for i, (src, dst) in enumerate(
            ((bias_ref, bias_far), (enc_ref, enc_far), (dec_ref, dec_far))
        )
    ]
    for copy in weights:
        copy.start()
    def relay(distance):
        @pl.loop(0, SUBS)
        def _(s):
            for way in (1, -1):
                @pl.when(has_next(-way * distance))
                def _():
                    q = place - way * distance
                    x_copy(q, s, way, False).wait_recv()

                    @pl.when(has_next(way))
                    def _():
                        x_copy(q, s, way, False).start()

    held[place] = x_ref[...]
    relay(1)

    for copy in weights:
        copy.wait_recv()

    def forward(q):
        data = held[q, :, :features]
        active = held[q, :, features:]
        block = lax.broadcasted_iota(jnp.int32, (active.shape[1], half), 0)
        column = lax.broadcasted_iota(jnp.int32, (active.shape[1], half), 1)
        blocks = half // BS
        for h, (weight, bias, owner) in enumerate(
            ((enc_ref, bias_ref, dict_at), (enc_far, bias_far, far))
        ):
            chosen = jnp.where(block == owner * blocks + column // BS, 1.0, 0.0).astype(bf16)
            mask = jnp.dot(active, chosen, preferred_element_type=f32) > 0.5
            pre = lax.dot_general(
                data, weight[...], (((1,), (1,)), ((), ())), preferred_element_type=f32
            )
            value, bend = gelu_and_slope(pre + bias[0:1, :])
            latent[q, :, h * half : (h + 1) * half] = jnp.where(mask, value, 0.0).astype(bf16)
            slope[q, :, h * half : (h + 1) * half] = jnp.where(mask, bend, 0.0)

    def decoded(q, columns):
        return jnp.dot(
            latent[q, :, :half], dec_ref[:, columns], preferred_element_type=f32
        ) + jnp.dot(latent[q, :, half:], dec_far[:, columns], preferred_element_type=f32)

    wide = 1024

    def each_columns(body):
        @pl.loop(0, features // wide)
        def _(i):
            body(pl.ds(pl.multiple_of(i * wide, wide), wide))

    forward(place)

    def keep_total(columns):
        total[:, columns] = decoded(place, columns) + dbias_ref[:, columns]

    each_columns(keep_total)

    @pl.loop(1, places)
    def _(distance):
        @pl.when(distance > 1)
        def _():
            relay(distance)

        @pl.loop(0, 2)
        def _(turn):
            way = 1 - 2 * turn
            q = place - way * distance

            @pl.when(jnp.logical_and(q >= 0, q < places))
            def _():
                forward(q)

                def keep_part(columns):
                    part[q, :, columns] = decoded(q, columns).astype(bf16)

                each_columns(keep_part)

                @pl.when(jnp.logical_not(has_next(way)))
                def _():
                    @pl.loop(0, SUBS)
                    def _(s):
                        p_copy(q, s, -way).start()

    def finish(s):
        here = part_rows(s)
        full = total[here, :]
        rebuilt_ref[here, :] = full.astype(bf16)
        res[place, here, :] = ((full - act_ref[here, :].astype(f32)) * LOSS_SCALE).astype(bf16)
        for way in (1, -1):
            @pl.when(has_next(way))
            def _():
                r_copy(place, s, way).start()

    ahead = jnp.where(place < places // 2, 1, -1)

    def add_own(s, way):
        here = part_rows(s)
        p_copy(place, s, way).wait_recv()
        total[here, :] += incoming[(way + 1) // 2, place, here, :].astype(f32)

    def pass_on(q, s, way):
        here = part_rows(s)
        p_copy(q, s, way).wait_recv()
        part[q, here, :] = (
            part[q, here, :].astype(f32) + incoming[(way + 1) // 2, q, here, :].astype(f32)
        ).astype(bf16)
        p_copy(q, s, way).start()

    @pl.when(inside)
    def _():
        @pl.loop(0, SUBS)
        def _(s):
            add_own(s, ahead)

        @pl.loop(0, SUBS)
        def _(s):
            pass_on(place + ahead, s, ahead)

    @pl.loop(0, SUBS)
    def _(s):
        add_own(s, -ahead)
        finish(s)

    @pl.when(inside)
    def _():
        @pl.loop(0, SUBS)
        def _(s):
            pass_on(place + 2 * ahead, s, ahead)
            pass_on(place - ahead, s, -ahead)

    def backward(q):
        for h, weight in enumerate((dec_ref, dec_far)):
            span = slice(h * half, (h + 1) * half)
            up = lax.dot_general(
                res[q], weight[...], (((1,), (1,)), ((), ())), preferred_element_type=f32
            )
            slope[q, :, span] = slope[q, :, span] * up

    def take_residual(q, s):
        way = jnp.where(q < place, 1, -1)
        r_copy(q, s, way).wait_recv()

        @pl.when(has_next(way))
        def _():
            r_copy(q, s, way).start()

    low = place < places // 2
    first = jnp.where(low, place + 1, place - 1)
    second = jnp.where(low, 2 - 2 * place, 7 - 2 * place)
    third = jnp.where(low, 3, 0)

    @pl.loop(0, SUBS)
    def _(s):
        take_residual(first, s)

    backward(place)
    backward(first)

    @pl.loop(0, SUBS)
    def _(s):
        take_residual(second, s)
        take_residual(third, s)

    @pl.loop(0, 2)
    def _(turn):
        backward(jnp.where(turn == 0, second, third))

    tile = 256

    def near_copy(g, k):
        return remote(
            near_out.at[g, k], near_in.at[g, k], n_send.at[g, k], n_recv.at[g, k], (row, far)
        )

    def row_copy(g, k):
        return remote(
            row_out.at[g, k], row_in.at[g, k], g_send.at[g, k], g_recv.at[g, k],
            ((row + k + 1) % row_size, dict_at),
        )

    for g, left in enumerate((res, held)):
        @pl.loop(0, row_size + 1)
        def _(k):
            @pl.when(k < row_size)
            def _():
                base = (row + k + 1) % row_size * slab

                @pl.loop(0, slab // tile)
                def _(i):
                    columns = pl.ds(pl.multiple_of(base + i * tile, tile), tile)
                    lefts = left[:, :, columns].reshape(places * rows, tile)
                    if g == 0:
                        rights = latent[...].reshape(places * rows, 2 * half)
                    else:
                        rights = slope[...].reshape(places * rows, 2 * half).astype(bf16)
                    product = lax.dot_general(
                        lefts, rights, (((0,), (0,)), ((), ())), preferred_element_type=f32
                    )
                    at = pl.ds(pl.multiple_of(i * tile, tile), tile)
                    acc[k % 2, at, :] = product[:, :half]
                    near_out[g, k, at, :] = product[:, half:].astype(bf16)

                near_copy(g, k).start()

            @pl.when(k > 0)
            def _():
                near_copy(g, k - 1).wait_recv()
                both = acc[(k - 1) % 2] + near_in[g, k - 1].astype(f32)

                @pl.when(k < row_size)
                def _():
                    row_out[g, k - 1] = both.astype(bf16)
                    row_copy(g, k - 1).start()

                @pl.when(k == row_size)
                def _():
                    fin[g] = both

    for g, out in enumerate((dec_grad_ref, enc_grad_ref)):
        for k in range(row_size - 1):
            row_copy(g, k).wait_recv()
        out[...] = (
            fin[g] + row_in[g, 0].astype(f32) + row_in[g, 1].astype(f32) + row_in[g, 2].astype(f32)
        ).astype(bf16)

    for copy in weights:
        copy.wait_send()

    @pl.loop(0, SUBS)
    def _(s):
        for way in (1, -1):
            @pl.when(has_next(way))
            def _():
                x_copy(place, s, way, True).wait_send()
                r_copy(place, s, way).wait_send()

                @pl.loop(0, places)
                def _(q):
                    @pl.when((q - place) * way < 0)
                    def _():
                        x_copy(q, s, way, False).wait_send()
                        r_copy(q, s, way).wait_send()

                    @pl.when((q - place) * way > 0)
                    def _():
                        p_copy(q, s, way).wait_send()

    for g in range(2):
        for k in range(row_size):
            near_copy(g, k).wait_send()
        for k in range(row_size - 1):
            row_copy(g, k).wait_send()


def fused_on_device(activations, block_ids, enc_weight, enc_bias, dec_weight, dec_bias):
    rows, features = activations.shape
    half = enc_weight.shape[0]
    places = lax.axis_size("dict") // 2
    row_size = lax.axis_size("row")
    slab = features // row_size
    f32, bf16 = jnp.float32, jnp.bfloat16
    shifted = (activations.astype(f32) - dec_bias[None, :]).astype(bf16)
    active = jnp.any(
        block_ids[:, :, None] == jnp.arange(128, dtype=jnp.int32)[None, None, :], axis=1
    ).astype(bf16)
    data = jnp.concatenate([shifted, active], axis=1)
    bias = jnp.broadcast_to(enc_bias[None, :], (8, half))
    dma = pltpu.SemaphoreType.DMA
    rebuilt, enc_grad, dec_grad = pl.pallas_call(
        step_kernel,
        out_shape=(
            jax.ShapeDtypeStruct((rows, features), bf16),
            jax.ShapeDtypeStruct((slab, half), bf16),
            jax.ShapeDtypeStruct((slab, half), bf16),
        ),
        in_specs=[pl.BlockSpec(memory_space=pltpu.VMEM)] * 6,
        out_specs=[pl.BlockSpec(memory_space=pltpu.VMEM)] * 3,
        scratch_shapes=[
            pltpu.VMEM((places, rows, features + 128), bf16),
            pltpu.VMEM((places, rows, features), bf16),
            pltpu.VMEM((half, features), bf16),
            pltpu.VMEM((half, features), bf16),
            pltpu.VMEM((8, half), f32),
            pltpu.VMEM((places, rows, features), bf16),
            pltpu.VMEM((rows, features), f32),
            pltpu.VMEM((2, places, rows, features), bf16),
            pltpu.VMEM((places, rows, 2 * half), bf16),
            pltpu.VMEM((places, rows, 2 * half), f32),
            pltpu.VMEM((2, slab, half), f32),
            pltpu.VMEM((2, slab, half), f32),
            pltpu.VMEM((2, row_size, slab, half), bf16),
            pltpu.VMEM((2, row_size, slab, half), bf16),
            pltpu.VMEM((2, row_size - 1, slab, half), bf16),
            pltpu.VMEM((2, row_size - 1, slab, half), bf16),
            dma((3,)), dma((3,)),
            dma((2, places, SUBS)), dma((places, SUBS)),
            dma((places, SUBS)), dma((2, places, SUBS)),
            dma((2, places, SUBS)), dma((places, SUBS)),
            dma((2, row_size)), dma((2, row_size)),
            dma((2, row_size - 1)), dma((2, row_size - 1)),
        ],
        compiler_params=pltpu.CompilerParams(
            collective_id=0, has_side_effects=True, vmem_limit_bytes=67043328
        ),
    )(data, activations, bias, dec_bias[None, :], enc_weight, dec_weight)
    return (rebuilt, enc_grad, dec_grad)


def solution(mesh):
    short_chain = mesh.shape["dict"] == 8 and mesh.shape["row"] == 4
    return jax.shard_map(
        fused_on_device if short_chain else on_device,
        mesh=mesh,
        in_specs=(
            P(("row", "dict"), None),
            P(("row", "dict"), None),
            P("dict", None),
            P("dict"),
            P("dict", None),
            P(),
        ),
        out_specs=(P(("row", "dict"), None), P("row", "dict"), P("row", "dict")),
        check_vma=False,
    )
```
